512 devices in a mesh: row: 32 (over x, y), col: 16 (over z, core).
Axes of the slice: x: 4, y: 8, z: 8, core: 2. Of those that a mesh axis runs over, the one named last changes fastest.
Arguments:
- matrix: float32 [8192, 8192], P('row', 'col'), may hold values from -6 to 6
- panel: float32 [8192, 128], P('col'), may hold values from -6 to 6
Outputs:
- updated: float32 [8192, 8192], P('row', 'col')
- band: float32 [128, 128], replicated
The draws below stay inside these ranges and needn't reach their ends.
All inputs are finite; a program needn't handle non-finite values.
Results may differ from the reference program's by a relative error of at most 0.0002.
Values sent between devices are 32-bit elements; how exact they have to be, the bound alone decides.
A program may use at most 64 MiB of HBM per device.

```python
import jax
import jax.numpy as jnp
from jax import lax

B = 128
ORDER = 8192


def steps_of(own_key, shape, cuts, smallest, largest):
    gain = 1.0
    for dim, parts in cuts:
        draws = jax.random.uniform(jax.random.fold_in(jax.random.fold_in(own_key, 6), dim), (parts,), jnp.float32, smallest / len(cuts), largest / len(cuts))
        gain = gain * jnp.repeat(jnp.exp(draws), shape[dim] // parts).reshape((-1,) + (1,) * (len(shape) - 1 - dim))
    return gain


def centred(key, shape, deviation, most, pieces=(), dtype=jnp.bfloat16):
    level = steps_of(key, shape, pieces, -0.22, 0.18) if pieces else 1.0
    result = jax.random.normal(key, shape, jnp.float32) * deviation * level
    return jnp.minimum(jnp.maximum(result, -most), most).astype(dtype)


def setup_inputs(seed: int = 0) -> dict:
    keys = jax.random.split(jax.random.key(seed), 3)
    return {
        "matrix": centred(keys[0], (ORDER, ORDER), 1.0, 6.0, ((0, 32), (1, 16)), jnp.float32),
        "panel": centred(keys[1], (ORDER, B), 1.0, 6.0, ((0, 16),), jnp.float32),
    }


def multiply(left_mat, right_mat):
    return jnp.dot(left_mat, right_mat, precision=lax.Precision.HIGHEST)

def reference(matrix, panel):
    width = panel.shape[1]
    gram = multiply(panel.T, panel)
    upper = jnp.linalg.cholesky(gram).T
    first = panel[:width]
    refl = panel + jnp.pad(upper, ((0, panel.shape[0] - width), (0, 0)))
    inv_upper = jnp.linalg.inv(upper)
    coupling = jnp.linalg.solve(upper + first, inv_upper.T)
    right = multiply(matrix, refl)
    left = multiply(refl.T, matrix)
    curv = multiply(refl.T, right)
    applied = multiply(coupling.T, left)
    second = multiply(right - multiply(refl, multiply(coupling.T, curv)), coupling)
    updated = matrix - multiply(refl, applied) - multiply(second, refl.T)
    return (updated, -upper)
```

```python
import functools

import jax
import jax.numpy as jnp
from jax import lax
from jax.experimental import pallas as pl
from jax.experimental.pallas import tpu as pltpu
from jax.sharding import PartitionSpec as P

F = jnp.float32
MESH = pl.DeviceIdType.MESH
NX, NY, NC = 4, 8, 16


def dot(a, b, ca=1, cb=0):
    return lax.dot_general(
        a, b, (((ca,), (cb,)), ((), ())), precision=lax.Precision.HIGHEST, preferred_element_type=F
    )


def split(v):
    high = v.astype(jnp.bfloat16).astype(F)
    rest = v - high
    mid = rest.astype(jnp.bfloat16).astype(F)
    return high, mid, rest - mid


def dot_short(a, b):
    ah, am, al = split(a)
    bh, bm, bl = split(b)
    left = jnp.concatenate([ah, ah, am, am, ah, al], 0).astype(jnp.bfloat16)
    right = jnp.concatenate([bh, bm, bh, bm, bl, bh], 0).astype(jnp.bfloat16)
    return lax.dot_general(left, right, (((0,), (0,)), ((), ())), preferred_element_type=F)


def spread(v, i):
    return jnp.broadcast_to(v[i : i + 1, :], v.shape)


def identity(n):
    return (
        lax.broadcasted_iota(jnp.int32, (n, n), 0) == lax.broadcasted_iota(jnp.int32, (n, n), 1)
    ).astype(F)


def factor(m_ref, hooks):
    n = m_ref.shape[0]
    sub = lax.broadcasted_iota(jnp.int32, (8, n), 0)
    for b in range(n // 8):
        lo = 8 * b
        left = m_ref[lo : lo + 8, :n]
        right = m_ref[lo : lo + 8, n:]
        cols = [jnp.broadcast_to(left[:, lo + k : lo + k + 1], (8, n)) for k in range(8)]
        pivots = jnp.ones((8, n), F)
        for i in range(8):
            pivot = spread(cols[i], i)
            pivots = jnp.where(sub == i, pivot, pivots)
            if i < 7:
                mult = jnp.where(sub > i, cols[i] / pivot, 0.0)
                for k in range(i + 1, 8):
                    cols[k] = cols[k] - mult * spread(cols[k], i)
                left = left - mult * spread(left, i)
                right = right - mult * spread(right, i)
        scale = lax.rsqrt(pivots)
        left = left * scale
        both = jnp.concatenate([left, right * scale], 1)
        m_ref[lo : lo + 8, :] = both
        if lo + 8 < n:
            m_ref[lo + 8 :, :] = m_ref[lo + 8 :, :] - dot_short(left, both)[lo + 8 :]
        if b in hooks:
            hooks[b]()


def invert(m_ref, hooks):
    n = m_ref.shape[0]
    sub = lax.broadcasted_iota(jnp.int32, (8, n), 0)
    for b in range(n // 8):
        lo = 8 * b
        left = m_ref[lo : lo + 8, :n]
        right = m_ref[lo : lo + 8, n:]
        cols = [jnp.broadcast_to(left[:, lo + k : lo + k + 1], (8, n)) for k in range(8)]
        for i in range(8):
            inverse = 1.0 / spread(cols[i], i)
            mult = jnp.where(sub == i, 1.0 - inverse, cols[i] * inverse)
            for k in range(i + 1, 8):
                cols[k] = cols[k] - mult * spread(cols[k], i)
            left = left - mult * spread(left, i)
            right = right - mult * spread(right, i)
        both = jnp.concatenate([left, right], 1)
        parts = [both]
        if lo:
            parts.insert(0, jnp.zeros((lo, 2 * n), F))
        if lo + 8 < n:
            parts.append(jnp.zeros((n - lo - 8, 2 * n), F))
        m_ref[...] = m_ref[...] - dot(m_ref[:, :n], jnp.concatenate(parts, 0))
        m_ref[lo : lo + 8, :] = both
        if b in hooks:
            hooks[b]()


def kernel(
    a_ref, p_ref, out_ref, band_ref,
    prow, gsrc, grecv, pone, gall, xsrc, xrecv, aleft, xall,
    lsrc, lxrecv, lysrc, lyrecv, tsrc, tblock, tchunk, mall, zown, zy, zx, zall, work, work2,
    zsend, zrecv, xsend, xrecv_sem, ysend, yrecv_sem, psend, precv,
):
    n = p_ref.shape[1]
    rix, cix = lax.axis_index("row"), lax.axis_index("col")
    x, y = lax.div(rix, NY), lax.rem(rix, NY)
    core = lax.rem(cix, 2)

    def zpeer(k):
        return lax.rem(cix + k, NC)

    def xpeer(k):
        return lax.rem(x + k, NX) * NY + y

    def ypeer(k):
        return x * NY + lax.rem(y + k, NY)

    def zcopy(ph, k, src, dst):
        return pltpu.make_async_remote_copy(
            src_ref=src, dst_ref=dst, send_sem=zsend.at[ph, k], recv_sem=zrecv.at[ph, k],
            device_id={"col": zpeer(k)}, device_id_type=MESH)

    def xcopy(ph, k, src, dst):
        return pltpu.make_async_remote_copy(
            src_ref=src, dst_ref=dst, send_sem=xsend.at[ph, k], recv_sem=xrecv_sem.at[ph, k],
            device_id={"row": xpeer(k)}, device_id_type=MESH)

    def ycopy(ph, k, src, dst):
        return pltpu.make_async_remote_copy(
            src_ref=src, dst_ref=dst, send_sem=ysend.at[ph, k], recv_sem=yrecv_sem.at[ph, k],
            device_id={"row": ypeer(k)}, device_id_type=MESH)

    def zloop(body):
        def step(j, _):
            half = lax.div(j + 1, 2)
            body(NC // 2 + jnp.where(lax.rem(j, 2) == 1, half, -half))
            return 0
        lax.fori_loop(0, NC - 1, step, 0)

    def rows(ref, index, count):
        return ref.at[pl.ds(pl.multiple_of(index * count, count), count)]

    barrier = pltpu.get_barrier_semaphore()
    zloop(lambda k: pl.semaphore_signal(barrier, inc=1, device_id={"col": zpeer(k)}, device_id_type=MESH))
    for k in range(1, NX):
        pl.semaphore_signal(barrier, inc=1, device_id={"row": xpeer(k)}, device_id_type=MESH)
    for k in range(1, NY):
        pl.semaphore_signal(barrier, inc=1, device_id={"row": ypeer(k)}, device_id_type=MESH)
    pl.semaphore_wait(barrier, NC - 1 + NX - 1 + NY - 1)

    owner = lax.div(rix, 2)
    base = lax.rem(rix, 2) * 256
    oz = lax.div(owner, 2)
    z = lax.div(cix, 2)

    def pcopy(slot, half_src, src, peer):
        return pltpu.make_async_remote_copy(
            src_ref=src, dst_ref=rows(prow, half_src, 128), send_sem=psend.at[slot], recv_sem=precv.at[half_src],
            device_id={"col": peer}, device_id_type=MESH)

    def psource(half):
        return p_ref.at[pl.ds(pl.multiple_of(base + half * 128, 128), 128)]

    @pl.when(cix == owner)
    def _():
        def step(j, _):
            half = lax.div(j + 1, 2)
            dz = 4 + jnp.where(lax.rem(j, 2) == 1, half, -half)
            chip = lax.rem(z + dz, 8)
            for h in range(2):
                pcopy(2 * dz + h, h, psource(h), chip * 2 + h).start()
            return 0
        lax.fori_loop(0, 7, step, 0)
        for h in range(2):
            pcopy(h, h, psource(h), z * 2 + 1 - core).start()
        prow[...] = p_ref[pl.ds(pl.multiple_of(base, 256), 256), :]

    @pl.when(cix == 0)
    def _():
        zloop(lambda k: zcopy(0, k, rows(p_ref, zpeer(k), 8), pone).start())
        zloop(lambda k: zcopy(1, k, a_ref.at[pl.ds(pl.multiple_of(zpeer(k) * 16, 16), 16), pl.ds(0, 128)], aleft).start())
        pone[...] = p_ref[0:8, :]
        aleft[...] = a_ref[0:16, 0:128]

    gsrc[...] = dot(p_ref[...], p_ref[...], 0, 0)
    zloop(lambda k: zcopy(2, k, rows(gsrc, zpeer(k), 8), grecv.at[cix]).start())
    grecv[cix] = gsrc[pl.ds(pl.multiple_of(cix * 8, 8), 8), :]

    xsrc[...] = dot(a_ref[...], p_ref[...])
    zloop(lambda k: zcopy(3, k, rows(xsrc, zpeer(k), 16), xrecv.at[cix]).start())
    xrecv[cix] = xsrc[pl.ds(pl.multiple_of(cix * 16, 16), 16), :]

    @pl.when(rix == 0)
    def _():
        tsrc[...] = a_ref[0:128, :].T
        for k in range(1, NX):
            xcopy(0, k, rows(tsrc, k, 128), tblock).start()
        tblock[...] = tsrc[0:128, :]

    @pl.when(cix != 0)
    def _():
        zcopy(0, cix, pone, pone).wait_recv()
    zloop(lambda k: zcopy(2, k, grecv.at[0], grecv.at[0]).wait_recv())
    gall[cix, :, :n] = jnp.sum(grecv[...], axis=0)
    gall[cix, :, n:] = pone[...]
    zloop(lambda k: zcopy(4, k, gall.at[cix], gall.at[cix]).start())

    @pl.when(z != oz)
    def _():
        pcopy(0, core, rows(prow, core, 128), 0).wait_recv()
        pcopy(0, core, rows(prow, core, 128), z * 2 + 1 - core).start()
        pcopy(0, 1 - core, rows(prow, 1 - core, 128), 0).wait_recv()

    @pl.when((z == oz) & (cix != owner))
    def _():
        for h in range(2):
            pcopy(0, h, rows(prow, h, 128), 0).wait_recv()

    lsrc[...] = dot(a_ref[...], prow[...], 0, 0)
    for k in range(1, NX):
        xcopy(1, k, rows(lsrc, lax.rem(x + k, NX), 128), lxrecv.at[x]).start()
    lxrecv[x] = lsrc[pl.ds(pl.multiple_of(x * 128, 128), 128), :]

    @pl.when(cix != 0)
    def _():
        zcopy(1, cix, aleft, aleft).wait_recv()
    zloop(lambda k: zcopy(3, k, xrecv.at[0], xrecv.at[0]).wait_recv())
    xall[cix, :, :n] = jnp.sum(xrecv[...], axis=0)
    xall[cix, :, n:] = aleft[...]
    zloop(lambda k: zcopy(5, k, xall.at[cix], xall.at[cix]).start())

    @pl.when(y == 0)
    def _():
        @pl.when(x != 0)
        def _():
            xcopy(0, x, tblock, tblock).wait_recv()
        for k in range(1, NY):
            ycopy(0, k, rows(tblock, k, 16), tchunk).start()
        tchunk[...] = tblock[0:16, :]

    zloop(lambda k: zcopy(4, k, gall.at[0], gall.at[0]).wait_recv())
    work[:, :n] = gall[...].reshape(n, 2 * n)[:, :n]
    work[:, n:] = identity(n)

    def reduce_x():
        for k in range(1, NX):
            xcopy(1, k, lxrecv.at[0], lxrecv.at[0]).wait_recv()
        lysrc[...] = jnp.sum(lxrecv[...], axis=0)
        for k in range(1, NY):
            ycopy(1, k, rows(lysrc, lax.rem(y + k, NY), 16), lyrecv.at[y]).start()
        lyrecv[y] = lysrc[pl.ds(pl.multiple_of(y * 16, 16), 16), :]

    factor(work, {9: reduce_x})
    eye = identity(n)
    upper_mask = lax.broadcasted_iota(jnp.int32, (n, n), 0) <= lax.broadcasted_iota(jnp.int32, (n, n), 1)
    band_ref[...] = jnp.where(upper_mask, -work[:, :n], 0.0)
    first = (cix == 0).astype(F)
    top = (rix == 0).astype(F)
    t = work[:, n:]
    yrow = dot(prow[...], t, 1, 1)
    yrow = jnp.concatenate([yrow[:n] + top * eye, yrow[n:]], 0)
    work2[:, :n] = dot(gall[...].reshape(n, 2 * n)[:, n:], t, 1, 1) + eye
    work2[:, n:] = eye

    zloop(lambda k: zcopy(5, k, xall.at[0], xall.at[0]).wait_recv())
    xa = xall[...].reshape(256, 2 * n)
    nrow = dot(xa[:, :n], t, 1, 1) + xa[:, n:]
    xsrc2 = dot(yrow, nrow, 0, 0)
    zown[...] = xsrc2
    zy[y] = zown[pl.ds(pl.multiple_of(cix * 8, 8), 8), :]
    for k in range(1, NY):
        ycopy(2, k, zy.at[y], zy.at[y]).start()

    def gather_y():
        @pl.when(y != 0)
        def _():
            ycopy(0, y, tchunk, tchunk).wait_recv()
        for k in range(1, NY):
            ycopy(1, k, lyrecv.at[0], lyrecv.at[0]).wait_recv()
        mall[x, pl.ds(pl.multiple_of(y * 16, 16), 16), :] = (
            dot(jnp.sum(lyrecv[...], axis=0), work[:, n:], 1, 1) + tchunk[...]
        )
        part = mall.at[x, pl.ds(pl.multiple_of(y * 16, 16), 16)]
        for k in range(1, NY):
            ycopy(3, k, part, part).start()

    def z_x():
        for k in range(1, NY):
            ycopy(2, k, zy.at[0], zy.at[0]).wait_recv()
        zx[x] = jnp.sum(zy[...], axis=0)
        for k in range(1, NX):
            xcopy(2, k, zx.at[x], zx.at[x]).start()

    def z_col():
        for k in range(1, NX):
            xcopy(2, k, zx.at[0], zx.at[0]).wait_recv()
        zall[cix] = jnp.sum(zx[...], axis=0)
        zloop(lambda k: zcopy(6, k, zall.at[cix], zall.at[cix]).start())

    def gather_x():
        part = mall.at[0, pl.ds(0, 16)]
        for k in range(1, NY):
            ycopy(3, k, part, part).wait_recv()
        for k in range(1, NX):
            xcopy(3, k, mall.at[x], mall.at[x]).start()

    invert(work2, {2: gather_y, 7: z_x, 12: z_col, 13: gather_x})
    s = work2[:, n:]
    ycol = dot(p_ref[...], t, 1, 1)
    ycol = jnp.concatenate([ycol[:n] + first * eye, ycol[n:]], 0)
    vt = dot(ycol, s, 1, 1)
    ys = dot(yrow, s, 1, 1)
    out_ref[...] = a_ref[...] - dot(nrow, vt, 1, 1)
    zloop(lambda k: zcopy(6, k, zall.at[0], zall.at[0]).wait_recv())
    zv = dot(vt, zall[...].reshape(n, n), 1, 1)
    for k in range(1, NX):
        xcopy(3, k, mall.at[0], mall.at[0]).wait_recv()
    out_ref[...] = out_ref[...] - dot(ys, mall[...].reshape(512, n) - zv, 1, 1)

    @pl.when(cix == owner)
    def _():
        lax.fori_loop(0, 16, lambda k, _: (pcopy(k, 0, psource(0), 0).wait_send(), 0)[1], 0)

    @pl.when(z != oz)
    def _():
        pcopy(0, core, rows(prow, core, 128), 0).wait_send()

    @pl.when(cix == 0)
    def _():
        zloop(lambda k: zcopy(0, k, pone, pone).wait_send())
        zloop(lambda k: zcopy(1, k, aleft, aleft).wait_send())
    for ph, ref in ((2, grecv), (3, xrecv), (4, gall), (5, xall), (6, zall)):
        zloop(lambda k: zcopy(ph, k, ref.at[0], ref.at[0]).wait_send())

    @pl.when(rix == 0)
    def _():
        for k in range(1, NX):
            xcopy(0, k, tblock, tblock).wait_send()

    @pl.when(y == 0)
    def _():
        for k in range(1, NY):
            ycopy(0, k, tchunk, tchunk).wait_send()
    for ph, ref in ((1, lxrecv), (2, zx), (3, mall)):
        for k in range(1, NX):
            xcopy(ph, k, ref.at[0], ref.at[0]).wait_send()
    for ph, ref in ((1, lyrecv.at[0]), (2, zy.at[0]), (3, mall.at[0, pl.ds(0, 16)])):
        for k in range(1, NY):
            ycopy(ph, k, ref, ref).wait_send()


def per_device(matrix, panel):
    vm = lambda *shape: pltpu.VMEM(shape, F)
    return pl.pallas_call(
        kernel,
        out_shape=(jax.ShapeDtypeStruct((256, 512), F), jax.ShapeDtypeStruct((128, 128), F)),
        in_specs=[pl.BlockSpec(memory_space=pltpu.VMEM)] * 2,
        out_specs=(pl.BlockSpec(memory_space=pltpu.VMEM),) * 2,
        scratch_shapes=[
            vm(256, 128), vm(128, 128), vm(16, 8, 128), vm(8, 128), vm(16, 8, 256),
            vm(256, 128), vm(16, 16, 128), vm(16, 128), vm(16, 16, 256),
            vm(512, 128), vm(4, 128, 128), vm(128, 128), vm(8, 16, 128), vm(512, 128), vm(128, 128), vm(16, 128),
            vm(4, 128, 128), vm(128, 128), vm(8, 8, 128), vm(4, 8, 128), vm(16, 8, 128), vm(128, 256), vm(128, 256),
            pltpu.SemaphoreType.DMA((7, 16)), pltpu.SemaphoreType.DMA((7, 16)),
            pltpu.SemaphoreType.DMA((4, 4)), pltpu.SemaphoreType.DMA((4, 4)),
            pltpu.SemaphoreType.DMA((4, 8)), pltpu.SemaphoreType.DMA((4, 8)),
            pltpu.SemaphoreType.DMA((16,)), pltpu.SemaphoreType.DMA((2,)),
        ],
        compiler_params=pltpu.CompilerParams(collective_id=0, has_side_effects=True),
        name="panel_transform",
    )(matrix, panel)


def solution(mesh):
    placed = (P("row", "col"), P("col", None))
    return jax.shard_map(
        per_device, mesh=mesh, in_specs=placed, out_specs=(P("row", "col"), P()), check_vma=False
    )
```

```python
import functools

PLACE = {'p': 0, 'x': 1, 'pass': 2, 'l': 6, 'sx': 9, 'sp': 12, 'nd': 14, 'g1': (1, 7), 'g2': (2, 6), 'g3': (3, 5, 4)}
import jax
import jax.numpy as jnp
from jax import lax
from jax.experimental import pallas as pl
from jax.experimental.pallas import tpu as pltpu
from jax.sharding import PartitionSpec as P

F = jnp.float32
MESH = pl.DeviceIdType.MESH
NX, NY, NC = 4, 8, 16


def dot(a, b, ca=1, cb=0):
    return lax.dot_general(
        a, b, (((ca,), (cb,)), ((), ())), precision=lax.Precision.HIGHEST, preferred_element_type=F
    )


def split(v):
    high = v.astype(jnp.bfloat16).astype(F)
    rest = v - high
    mid = rest.astype(jnp.bfloat16).astype(F)
    return high, mid, rest - mid


def dot_short(a, b):
    ah, am, al = split(a)
    bh, bm, bl = split(b)
    left = jnp.concatenate([ah, ah, am, am, ah, al], 0).astype(jnp.bfloat16)
    right = jnp.concatenate([bh, bm, bh, bm, bl, bh], 0).astype(jnp.bfloat16)
    return lax.dot_general(left, right, (((0,), (0,)), ((), ())), preferred_element_type=F)


def spread(v, i):
    return jnp.broadcast_to(v[i : i + 1, :], v.shape)


def identity(n):
    return (
        lax.broadcasted_iota(jnp.int32, (n, n), 0) == lax.broadcasted_iota(jnp.int32, (n, n), 1)
    ).astype(F)


def factor(m_ref, hooks):
    n = m_ref.shape[0]
    sub = lax.broadcasted_iota(jnp.int32, (8, n), 0)
    for b in range(n // 8):
        lo = 8 * b
        left = m_ref[lo : lo + 8, :n]
        right = m_ref[lo : lo + 8, n:]
        cols = [jnp.broadcast_to(left[:, lo + k : lo + k + 1], (8, n)) for k in range(8)]
        pivots = jnp.ones((8, n), F)
        for i in range(8):
            pivot = spread(cols[i], i)
            pivots = jnp.where(sub == i, pivot, pivots)
            if i < 7:
                mult = jnp.where(sub > i, cols[i] / pivot, 0.0)
                for k in range(i + 1, 8):
                    cols[k] = cols[k] - mult * spread(cols[k], i)
                left = left - mult * spread(left, i)
                right = right - mult * spread(right, i)
        scale = lax.rsqrt(pivots)
        left = left * scale
        both = jnp.concatenate([left, right * scale], 1)
        m_ref[lo : lo + 8, :] = both
        if lo + 8 < n:
            m_ref[lo + 8 :, :] = m_ref[lo + 8 :, :] - dot_short(left, both)[lo + 8 :]
        if b in hooks:
            hooks[b]()


def inverse(q, doublings):
    eye = identity(q.shape[0])
    power = 0.5 * (eye - q)
    total = 0.5 * (eye + power)
    for _ in range(doublings - 1):
        power = dot(power, power)
        total = total + dot(total, power)
    return total


def kernel(
    a_hbm, p_hbm, out_ref, band_ref,
    a_ref, p_ref, prow, gsrc, grecv, pone, pall, gall, xsrc, xrecv, aleft, xall,
    lsrc, lxrecv, lysrc, lyrecv, tsrc, tblock, tchunk, mall, zown, zy, zx, zall, work, vts,
    zsend, zrecv, xsend, xrecv_sem, ysend, yrecv_sem, psend, precv, fsend, frecv, msem, asem, psem,
):
    n = p_ref.shape[1]
    rix, cix = lax.axis_index("row"), lax.axis_index("col")
    x, y = lax.div(rix, NY), lax.rem(rix, NY)
    z, core = lax.div(cix, 2), lax.rem(cix, 2)

    def zpeer(k):
        return lax.rem(cix + k, NC)

    def xpeer(k):
        return lax.rem(x + k, NX) * NY + y

    def ypeer(k):
        return x * NY + lax.rem(y + k, NY)

    def zcopy(ph, k, src, dst):
        return pltpu.make_async_remote_copy(
            src_ref=src, dst_ref=dst, send_sem=zsend.at[ph], recv_sem=zrecv.at[ph],
            device_id={"col": zpeer(k)}, device_id_type=MESH)

    def xcopy(ph, k, src, dst):
        return pltpu.make_async_remote_copy(
            src_ref=src, dst_ref=dst, send_sem=xsend.at[ph], recv_sem=xrecv_sem.at[ph],
            device_id={"row": xpeer(k)}, device_id_type=MESH)

    def ycopy(ph, k, src, dst):
        return pltpu.make_async_remote_copy(
            src_ref=src, dst_ref=dst, send_sem=ysend.at[ph], recv_sem=yrecv_sem.at[ph],
            device_id={"row": ypeer(k)}, device_id_type=MESH)

    def mcopy(k, src, dst):
        return pltpu.make_async_remote_copy(
            src_ref=src, dst_ref=dst, send_sem=ysend.at[3], recv_sem=msem.at[k],
            device_id={"row": ypeer(k)}, device_id_type=MESH)

    def fcopy(j, k, src, dst):
        return pltpu.make_async_remote_copy(
            src_ref=src, dst_ref=dst, send_sem=fsend.at[k], recv_sem=frecv.at[k],
            device_id={"row": xpeer(k)}, device_id_type=MESH)

    def zloop(body):
        for k in (8, 9, 7, 10, 6, 11, 5, 12, 4, 13, 3, 14, 2, 15, 1):
            body(k)

    def rows(ref, index, count):
        return ref.at[pl.ds(pl.multiple_of(index * count, count), count)]

    waits = {}

    def begin(name, recv, send):
        waits[name] = [recv, send]

    def recv(name):
        waits[name][0]()
        waits[name][0] = None

    def drain():
        for first_wait, last_wait in waits.values():
            if first_wait is not None:
                first_wait()
            last_wait()

    def landed(copy, ph, ref):
        return lambda: copy(ph, 1, ref, ref).wait_recv()

    def left(copy, ph, ref):
        return lambda: copy(ph, 1, ref, ref).wait_send()

    def group(name, copy, ph, ref):
        begin(name, landed(copy, ph, ref), left(copy, ph, ref))

    def only(cond, f):
        return lambda: pl.when(cond)(f)

    pin = [pltpu.make_async_copy(p_hbm.at[pl.ds(128 * k, 128)], p_ref.at[pl.ds(128 * k, 128)], psem.at[k]) for k in range(4)]
    ain = [pltpu.make_async_copy(a_hbm.at[pl.ds(64 * k, 64)], a_ref.at[pl.ds(64 * k, 64)], asem.at[k]) for k in range(4)]
    for copy in pin + ain:
        copy.start()
    barrier = pltpu.get_barrier_semaphore()
    zloop(lambda k: pl.semaphore_signal(barrier, inc=1, device_id={"col": zpeer(k)}, device_id_type=MESH))
    for k in range(1, NX):
        pl.semaphore_signal(barrier, inc=1, device_id={"row": xpeer(k)}, device_id_type=MESH)
    for k in range(1, NY):
        pl.semaphore_signal(barrier, inc=1, device_id={"row": ypeer(k)}, device_id_type=MESH)
    for copy in pin:
        copy.wait()
    gsrc[...] = dot(p_ref[...], p_ref[...], 0, 0)
    grecv[cix] = gsrc[pl.ds(pl.multiple_of(cix * 8, 8), 8), :]
    for copy in ain:
        copy.wait()
    xsrc[...] = dot(a_ref[...], p_ref[...])
    xrecv[cix] = xsrc[pl.ds(pl.multiple_of(cix * 16, 16), 16), :]
    pl.semaphore_wait(barrier, NC - 1 + NX - 1 + NY - 1)

    zloop(lambda k: zcopy(2, k, rows(gsrc, zpeer(k), 8), grecv.at[cix]).start())
    group("gram", zcopy, 2, grecv.at[pl.ds(0, 15)])

    owner = lax.div(rix, 2)
    base = lax.rem(rix, 2) * 256
    oz = lax.div(owner, 2)

    def pcopy(slot, half_src, src, peer):
        return pltpu.make_async_remote_copy(
            src_ref=src, dst_ref=src if src is a_ref else rows(prow, half_src, 128), send_sem=psend.at[slot], recv_sem=precv.at[half_src],
            device_id={"col": peer}, device_id_type=MESH)

    def psource(half):
        return p_ref.at[pl.ds(pl.multiple_of(base + half * 128, 128), 128)]

    def send_panel():
        @pl.when(cix == owner)
        def _():
            for dz in (4, 5, 3, 6, 2, 7, 1):
                chip = lax.rem(z + dz, 8)
                for h in range(2):
                    pcopy(h, h, psource(h), chip * 2 + h).start()
            for h in range(2):
                pcopy(h, h, psource(h), z * 2 + 1 - core).start()
            prow[...] = p_ref[pl.ds(pl.multiple_of(base, 256), 256), :]

    def pass_panel():
        @pl.when(z != oz)
        def _():
            pcopy(0, core, rows(prow, core, 128), 0).wait_recv()
            pcopy(2, core, rows(prow, core, 128), z * 2 + 1 - core).start()

    def prow_recv():
        @pl.when(z != oz)
        def _():
            pcopy(0, 1 - core, rows(prow, 1 - core, 128), 0).wait_recv()

        @pl.when((z == oz) & (cix != owner))
        def _():
            for h in range(2):
                pcopy(0, h, rows(prow, h, 128), 0).wait_recv()

    def prow_send():
        @pl.when(cix == owner)
        def _():
            for h in range(2):
                pcopy(h, h, a_ref, 0).wait_send()

        @pl.when(z != oz)
        def _():
            pcopy(2, core, rows(prow, core, 128), 0).wait_send()

    begin("prow", prow_recv, prow_send)

    def send_leading():
        @pl.when(cix == 0)
        def _():
            zloop(lambda k: zcopy(0, k, rows(p_ref, zpeer(k), 8), pone).start())
            zloop(lambda k: zcopy(1, k, a_ref.at[pl.ds(pl.multiple_of(zpeer(k) * 16, 16), 16), pl.ds(0, 128)], aleft).start())
            pone[...] = p_ref[0:8, :]
            aleft[...] = a_ref[0:16, 0:128]

    begin("pone", only(cix != 0, landed(zcopy, 0, pone)), only(cix == 0, left(zcopy, 0, p_ref.at[pl.ds(0, 120)])))
    begin("aleft", only(cix != 0, landed(zcopy, 1, aleft)), only(cix == 0, left(zcopy, 1, xrecv.at[pl.ds(0, 15)])))

    def send_x():
        zloop(lambda k: zcopy(3, k, rows(xsrc, zpeer(k), 16), xrecv.at[cix]).start())
        group("x", zcopy, 3, xrecv.at[pl.ds(0, 15)])

    if PLACE['p'] == 0:
        send_panel()
    if PLACE['x'] == 0:
        send_leading()
        send_x()

    recv("gram")
    gall[cix] = jnp.sum(grecv[...], axis=0)
    zloop(lambda k: zcopy(4, k, gall.at[cix], gall.at[cix]).start())
    group("gall", zcopy, 4, gall.at[pl.ds(0, 15)])
    if PLACE['p'] == 1:
        send_panel()
    if PLACE['x'] == 1:
        send_leading()
        send_x()

    @pl.when(rix == 0)
    def _():
        tsrc[...] = a_ref[0:128, :].T
        for k in range(1, NX):
            xcopy(0, k, rows(tsrc, k, 128), tblock).start()
        tblock[...] = tsrc[0:128, :]
    begin("tblock", only((y == 0) & (x != 0), landed(xcopy, 0, tblock)), only(rix == 0, left(xcopy, 0, lxrecv.at[pl.ds(0, 3)])))

    def send_l():
        recv("prow")
        for k in (2, 1, 3, 0):
            block = lax.rem(x + k, NX)
            part = dot(a_ref[:, pl.ds(pl.multiple_of(block * 128, 128), 128)], prow[...], 0, 0)
            if k:
                lsrc[block] = part
                xcopy(1, k, lsrc.at[block], lxrecv.at[x]).start()
            else:
                lxrecv[x] = part
        group("lx", xcopy, 1, lxrecv.at[pl.ds(0, 3)])

    def share_panel():
        recv("pone")
        pall[cix] = pone[...]
        zloop(lambda k: zcopy(7, k, pall.at[cix], pall.at[cix]).start())
        group("pall", zcopy, 7, pall.at[pl.ds(0, 15)])
        recv("tblock")

        @pl.when(y == 0)
        def _():
            for k in range(1, NY):
                ycopy(0, k, rows(tblock, k, 16), tchunk).start()
            tchunk[...] = tblock[0:16, :]
        begin("tchunk", only(y != 0, landed(ycopy, 0, tchunk)), only(y == 0, left(ycopy, 0, tblock.at[pl.ds(0, 112)])))

    def share_x():
        recv("aleft")
        recv("x")
        xall[cix, :, :n] = jnp.sum(xrecv[...], axis=0)
        xall[cix, :, n:] = aleft[...]
        zloop(lambda k: zcopy(5, k, xall.at[cix], xall.at[cix]).start())
        group("xall", zcopy, 5, xall.at[pl.ds(0, 15)])

    def at(name):
        for b, f in ((PLACE['pass'], pass_panel), (PLACE['l'], send_l), (PLACE['sx'], share_x), (PLACE['sp'], share_panel)):
            if b == name:
                f()

    at(-2)
    recv("gall")
    at(-1)
    work[:, :n] = gall[...].reshape(n, n)
    work[:, n:] = identity(n)
    factor(work, {b: functools.partial(at, b) for b in range(16)})
    at(16)

    recv("lx")
    lysrc[...] = jnp.sum(lxrecv[...], axis=0)
    for k in range(1, NY):
        ycopy(1, k, rows(lysrc, lax.rem(y + k, NY), 16), lyrecv.at[y]).start()
    lyrecv[y] = lysrc[pl.ds(pl.multiple_of(y * 16, 16), 16), :]
    group("ly", ycopy, 1, lyrecv.at[pl.ds(0, 7)])

    eye = identity(n)
    first = (cix == 0).astype(F)
    top = (rix == 0).astype(F)
    t = work[:, n:]
    yrow = dot(prow[...], t, 1, 1)
    yrow = jnp.concatenate([yrow[:n] + top * eye, yrow[n:]], 0)
    recv("xall")
    xa = xall[...].reshape(256, 2 * n)
    nrow = dot(xa[:, :n], t, 1, 1) + xa[:, n:]
    zown[...] = dot(yrow, nrow, 0, 0)
    zy[y] = zown[pl.ds(pl.multiple_of(cix * 8, 8), 8), :]
    for k in range(1, NY):
        ycopy(2, k, zy.at[y], zy.at[y]).start()
    group("zy", ycopy, 2, zy.at[pl.ds(0, 7)])
    recv("pall")
    s = inverse(dot(pall[...].reshape(n, n), t, 1, 1), PLACE['nd'])
    ycol = dot(p_ref[...], t, 1, 1)
    ycol = jnp.concatenate([ycol[:n] + first * eye, ycol[n:]], 0)
    upper = lax.broadcasted_iota(jnp.int32, (n, n), 0) <= lax.broadcasted_iota(jnp.int32, (n, n), 1)
    band_ref[...] = jnp.where(upper, -work[:, :n], 0.0)

    def gather_y():
        recv("tchunk")
        recv("ly")
        part = mall.at[x, pl.ds(pl.multiple_of(y * 16, 16), 16)]
        part[...] = dot(jnp.sum(lyrecv[...], axis=0), work[:, n:], 1, 1) + tchunk[...]
        for k in range(1, NY):
            mcopy(k, part, part).start()
        for k in range(1, NX):
            fcopy(0, k, part, part).start()
        for k in range(1, NY):
            begin(f"m{k}", mcopy(k, tchunk, tchunk).wait_recv, lambda: None)
        waits["m1"][1] = left(ycopy, 3, tblock.at[pl.ds(0, 112)])

    def z_x():
        recv("zy")
        zx[x] = jnp.sum(zy[...], axis=0)
        for k in range(1, NX):
            xcopy(2, k, zx.at[x], zx.at[x]).start()
        group("zx", xcopy, 2, zx.at[pl.ds(0, 3)])

    def z_col():
        recv("zx")
        zall[cix] = jnp.sum(zx[...], axis=0)
        zloop(lambda k: zcopy(6, k, zall.at[cix], zall.at[cix]).start())
        group("zall", zcopy, 6, zall.at[pl.ds(0, 15)])

    def gather_x(j):
        def go():
            part = mall.at[x, pl.ds(pl.multiple_of(lax.rem(y + NY - j, NY) * 16, 16), 16)]
            recv(f"m{j}")
            for k in range(1, NX):
                fcopy(j, k, part, part).start()
        return go

    gather_y()
    z_x()
    vt = dot(ycol, s, 1, 1)
    vts[...] = vt.reshape(4, n, n)
    ys = dot(yrow, s, 1, 1)
    for j in PLACE['g1']:
        gather_x(j)()
    z_col()
    for j in PLACE['g2']:
        gather_x(j)()
    out_ref[...] = a_ref[...] - dot(nrow, vt, 1, 1)
    for j in PLACE['g3']:
        gather_x(j)()
    recv("zall")
    zfull = zall[...].reshape(n, n)
    for k in (0, 1, 3, 2):
        block = lax.rem(x + NX - k, NX)
        if k:
            fcopy(0, k, mall.at[0], mall.at[0]).wait_recv()
        rest = mall[block] - dot(vts[block], zfull, 1, 1)
        at_block = pl.ds(pl.multiple_of(block * 128, 128), 128)
        out_ref[:, at_block] = out_ref[:, at_block] - dot(ys, rest, 1, 1)

    drain()
    for k in range(1, NX):
        fcopy(0, k, mall.at[0], mall.at[0]).wait_send()


def per_device(matrix, panel):
    keep = lambda v: pltpu.with_memory_space_constraint(v, pltpu.MemorySpace.HBM)
    vm = lambda *shape: pltpu.VMEM(shape, F)
    dma = lambda *shape: pltpu.SemaphoreType.DMA(shape)
    return pl.pallas_call(
        kernel,
        out_shape=(jax.ShapeDtypeStruct((256, 512), F), jax.ShapeDtypeStruct((128, 128), F)),
        in_specs=[pl.BlockSpec(memory_space=pltpu.MemorySpace.HBM)] * 2,
        out_specs=(pl.BlockSpec(memory_space=pltpu.VMEM),) * 2,
        scratch_shapes=[
            vm(256, 512), vm(512, 128),
            vm(256, 128), vm(128, 128), vm(16, 8, 128), vm(8, 128), vm(16, 8, 128), vm(16, 8, 128),
            vm(256, 128), vm(16, 16, 128), vm(16, 128), vm(16, 16, 256),
            vm(4, 128, 128), vm(4, 128, 128), vm(128, 128), vm(8, 16, 128), vm(512, 128), vm(128, 128), vm(16, 128),
            vm(4, 128, 128), vm(128, 128), vm(8, 8, 128), vm(4, 8, 128), vm(16, 8, 128), vm(128, 256), vm(4, 128, 128),
            dma(8), dma(8), dma(3), dma(3), dma(4), dma(4), dma(3), dma(2), dma(4), dma(4), dma(8),
            dma(4), dma(4),
        ],
        compiler_params=pltpu.CompilerParams(collective_id=0, has_side_effects=True, vmem_limit_bytes=16 << 20),
        name="panel_transform",
    )(keep(matrix), keep(panel))


def solution(mesh):
    placed = (P("row", "col"), P("col", None))
    return jax.shard_map(
        per_device, mesh=mesh, in_specs=placed, out_specs=(P("row", "col"), P()), check_vma=False
    )
```

```python
import functools

PLACE = {'p': 0, 'x': 1, 'pass': 1, 'l': 3, 'sx': 7, 'sp': 0, 'nd': 14, 'g1': (), 'g2': (1, 7), 'g3': (2, 6, 3, 5, 4)}
import jax
import jax.numpy as jnp
from jax import lax
from jax.experimental import pallas as pl
from jax.experimental.pallas import tpu as pltpu
from jax.sharding import PartitionSpec as P

F = jnp.float32
MESH = pl.DeviceIdType.MESH
NX, NY, NC = 4, 8, 16


def split(v):
    high = v.astype(jnp.bfloat16).astype(F)
    rest = v - high
    mid = rest.astype(jnp.bfloat16).astype(F)
    return high, mid, rest - mid


def dot(a, b, ca=1, cb=0):
    if ca == 0:
        return lax.dot_general(
            a, b, (((ca,), (cb,)), ((), ())), precision=lax.Precision.HIGHEST, preferred_element_type=F
        )
    ah, am, al = [v.astype(jnp.bfloat16) for v in split(a)]
    bh, bm, bl = [v.astype(jnp.bfloat16) for v in split(b)]
    left = jnp.concatenate([ah, ah, am, am, ah, al], ca)
    right = jnp.concatenate([bh, bm, bh, bm, bl, bh], cb)
    return lax.dot_general(left, right, (((ca,), (cb,)), ((), ())), preferred_element_type=F)


def dot_short(a, b):
    ah, am, al = split(a)
    bh, bm, bl = split(b)
    left = jnp.concatenate([ah, ah, am, am, ah, al], 0).astype(jnp.bfloat16)
    right = jnp.concatenate([bh, bm, bh, bm, bl, bh], 0).astype(jnp.bfloat16)
    return lax.dot_general(left, right, (((0,), (0,)), ((), ())), preferred_element_type=F)


def spread(v, i):
    return jnp.broadcast_to(v[i : i + 1, :], v.shape)


def identity(n):
    return (
        lax.broadcasted_iota(jnp.int32, (n, n), 0) == lax.broadcasted_iota(jnp.int32, (n, n), 1)
    ).astype(F)


def factor(m_ref, hooks):
    n = m_ref.shape[0]
    sub = lax.broadcasted_iota(jnp.int32, (8, n), 0)
    for b in range(n // 8):
        lo = 8 * b
        left = m_ref[lo : lo + 8, :n]
        right = m_ref[lo : lo + 8, n:]
        cols = [jnp.broadcast_to(left[:, lo + k : lo + k + 1], (8, n)) for k in range(8)]
        pivots = jnp.ones((8, n), F)
        for i in range(8):
            pivot = spread(cols[i], i)
            pivots = jnp.where(sub == i, pivot, pivots)
            if i < 7:
                mult = jnp.where(sub > i, cols[i] / pivot, 0.0)
                for k in range(i + 1, 8):
                    cols[k] = cols[k] - mult * spread(cols[k], i)
                left = left - mult * spread(left, i)
                right = right - mult * spread(right, i)
        scale = lax.rsqrt(pivots)
        left = left * scale
        both = jnp.concatenate([left, right * scale], 1)
        m_ref[lo : lo + 8, :] = both
        if lo + 8 < n:
            m_ref[lo + 8 :, :] = m_ref[lo + 8 :, :] - dot_short(left, both)[lo + 8 :]
        if b in hooks:
            hooks[b]()


def inverse(q, doublings):
    eye = identity(q.shape[0])
    power = 0.5 * (eye - q)
    total = 0.5 * (eye + power)
    for _ in range(doublings - 1):
        power = dot(power, power)
        total = total + dot(total, power)
    return total


def kernel(
    a_hbm, p_hbm, out_ref, band_ref,
    a_ref, p_ref, prow, gsrc, grecv, pone, pall, gall, xsrc, xrecv, aleft, xall,
    lsrc, lxrecv, lysrc, lyrecv, tsrc, tblock, tchunk, mall, zown, zy, zx, zall, work, vts,
    zsend, zrecv, xsend, xrecv_sem, ysend, yrecv_sem, psend, precv, fsend, frecv, msem, asem, psem,
):
    n = p_ref.shape[1]
    rix, cix = lax.axis_index("row"), lax.axis_index("col")
    x, y = lax.div(rix, NY), lax.rem(rix, NY)
    z, core = lax.div(cix, 2), lax.rem(cix, 2)

    def zpeer(k):
        return lax.rem(cix + k, NC)

    def xpeer(k):
        return lax.rem(x + k, NX) * NY + y

    def ypeer(k):
        return x * NY + lax.rem(y + k, NY)

    def zcopy(ph, k, src, dst):
        return pltpu.make_async_remote_copy(
            src_ref=src, dst_ref=dst, send_sem=zsend.at[ph], recv_sem=zrecv.at[ph],
            device_id={"col": zpeer(k)}, device_id_type=MESH)

    def xcopy(ph, k, src, dst):
        return pltpu.make_async_remote_copy(
            src_ref=src, dst_ref=dst, send_sem=xsend.at[ph], recv_sem=xrecv_sem.at[ph],
            device_id={"row": xpeer(k)}, device_id_type=MESH)

    def ycopy(ph, k, src, dst):
        return pltpu.make_async_remote_copy(
            src_ref=src, dst_ref=dst, send_sem=ysend.at[ph], recv_sem=yrecv_sem.at[ph],
            device_id={"row": ypeer(k)}, device_id_type=MESH)

    def mcopy(k, src, dst):
        return pltpu.make_async_remote_copy(
            src_ref=src, dst_ref=dst, send_sem=ysend.at[3], recv_sem=msem.at[k],
            device_id={"row": ypeer(k)}, device_id_type=MESH)

    def fcopy(j, k, src, dst):
        return pltpu.make_async_remote_copy(
            src_ref=src, dst_ref=dst, send_sem=fsend.at[k], recv_sem=frecv.at[k],
            device_id={"row": xpeer(k)}, device_id_type=MESH)

    def zloop(body):
        for k in (8, 9, 7, 10, 6, 11, 5, 12, 4, 13, 3, 14, 2, 15, 1):
            body(k)

    def rows(ref, index, count):
        return ref.at[pl.ds(pl.multiple_of(index * count, count), count)]

    waits = {}

    def begin(name, recv, send):
        waits[name] = [recv, send]

    def recv(name):
        waits[name][0]()
        waits[name][0] = None

    def drain():
        for first_wait, last_wait in waits.values():
            if first_wait is not None:
                first_wait()
            last_wait()

    def landed(copy, ph, ref):
        return lambda: copy(ph, 1, ref, ref).wait_recv()

    def left(copy, ph, ref):
        return lambda: copy(ph, 1, ref, ref).wait_send()

    def group(name, copy, ph, ref):
        begin(name, landed(copy, ph, ref), left(copy, ph, ref))

    def only(cond, f):
        return lambda: pl.when(cond)(f)

    pin = [pltpu.make_async_copy(p_hbm.at[pl.ds(128 * k, 128)], p_ref.at[pl.ds(128 * k, 128)], psem.at[k]) for k in range(4)]
    ain = [pltpu.make_async_copy(a_hbm.at[pl.ds(64 * k, 64)], a_ref.at[pl.ds(64 * k, 64)], asem.at[k]) for k in range(4)]
    for copy in pin + ain:
        copy.start()
    barrier = pltpu.get_barrier_semaphore()
    zloop(lambda k: pl.semaphore_signal(barrier, inc=1, device_id={"col": zpeer(k)}, device_id_type=MESH))
    for k in range(1, NX):
        pl.semaphore_signal(barrier, inc=1, device_id={"row": xpeer(k)}, device_id_type=MESH)
    for k in range(1, NY):
        pl.semaphore_signal(barrier, inc=1, device_id={"row": ypeer(k)}, device_id_type=MESH)
    for copy in pin:
        copy.wait()
    gsrc[...] = dot(p_ref[...], p_ref[...], 0, 0)
    grecv[cix] = gsrc[pl.ds(pl.multiple_of(cix * 8, 8), 8), :]
    for copy in ain:
        copy.wait()
    xsrc[...] = dot(a_ref[...], p_ref[...])
    xrecv[cix] = xsrc[pl.ds(pl.multiple_of(cix * 16, 16), 16), :]
    pl.semaphore_wait(barrier, NC - 1 + NX - 1 + NY - 1)

    zloop(lambda k: zcopy(2, k, rows(gsrc, zpeer(k), 8), grecv.at[cix]).start())
    group("gram", zcopy, 2, grecv.at[pl.ds(0, 15)])

    owner = lax.div(rix, 2)
    base = lax.rem(rix, 2) * 256
    oz = lax.div(owner, 2)

    def pcopy(slot, half_src, src, peer):
        return pltpu.make_async_remote_copy(
            src_ref=src, dst_ref=src if src is a_ref else rows(prow, half_src, 128), send_sem=psend.at[slot], recv_sem=precv.at[half_src],
            device_id={"col": peer}, device_id_type=MESH)

    def psource(half):
        return p_ref.at[pl.ds(pl.multiple_of(base + half * 128, 128), 128)]

    def send_panel():
        @pl.when(cix == owner)
        def _():
            for dz in (4, 5, 3, 6, 2, 7, 1):
                chip = lax.rem(z + dz, 8)
                for h in range(2):
                    pcopy(h, h, psource(h), chip * 2 + h).start()
            for h in range(2):
                pcopy(h, h, psource(h), z * 2 + 1 - core).start()
            prow[...] = p_ref[pl.ds(pl.multiple_of(base, 256), 256), :]

    def pass_panel():
        @pl.when(z != oz)
        def _():
            pcopy(0, core, rows(prow, core, 128), 0).wait_recv()
            pcopy(2, core, rows(prow, core, 128), z * 2 + 1 - core).start()

    def prow_recv():
        @pl.when(z != oz)
        def _():
            pcopy(0, 1 - core, rows(prow, 1 - core, 128), 0).wait_recv()

        @pl.when((z == oz) & (cix != owner))
        def _():
            for h in range(2):
                pcopy(0, h, rows(prow, h, 128), 0).wait_recv()

    def prow_send():
        @pl.when(cix == owner)
        def _():
            for h in range(2):
                pcopy(h, h, a_ref, 0).wait_send()

        @pl.when(z != oz)
        def _():
            pcopy(2, core, rows(prow, core, 128), 0).wait_send()

    begin("prow", prow_recv, prow_send)

    def send_leading():
        @pl.when(cix == 0)
        def _():
            zloop(lambda k: zcopy(0, k, rows(p_ref, zpeer(k), 8), pone).start())
            zloop(lambda k: zcopy(1, k, a_ref.at[pl.ds(pl.multiple_of(zpeer(k) * 16, 16), 16), pl.ds(0, 128)], aleft).start())
            pone[...] = p_ref[0:8, :]
            aleft[...] = a_ref[0:16, 0:128]

    begin("pone", only(cix != 0, landed(zcopy, 0, pone)), only(cix == 0, left(zcopy, 0, p_ref.at[pl.ds(0, 120)])))
    begin("aleft", only(cix != 0, landed(zcopy, 1, aleft)), only(cix == 0, left(zcopy, 1, xrecv.at[pl.ds(0, 15)])))

    def send_x():
        zloop(lambda k: zcopy(3, k, rows(xsrc, zpeer(k), 16), xrecv.at[cix]).start())
        group("x", zcopy, 3, xrecv.at[pl.ds(0, 15)])

    if PLACE['p'] == 0:
        send_panel()
    if PLACE['x'] == 0:
        send_leading()
        send_x()
    if PLACE['p'] == 2:
        send_panel()

    recv("gram")
    gall[cix] = jnp.sum(grecv[...], axis=0)
    zloop(lambda k: zcopy(4, k, gall.at[cix], gall.at[cix]).start())
    group("gall", zcopy, 4, gall.at[pl.ds(0, 15)])
    if PLACE['p'] == 1:
        send_panel()
    if PLACE['x'] == 1:
        send_leading()
        send_x()

    @pl.when(rix == 0)
    def _():
        tsrc[...] = a_ref[0:128, :].T
        for k in range(1, NX):
            xcopy(0, k, rows(tsrc, k, 128), tblock).start()
        tblock[...] = tsrc[0:128, :]
    begin("tblock", only((y == 0) & (x != 0), landed(xcopy, 0, tblock)), only(rix == 0, left(xcopy, 0, lxrecv.at[pl.ds(0, 3)])))

    def send_l():
        recv("prow")
        for k in (2, 1, 3, 0):
            block = lax.rem(x + k, NX)
            part = dot(a_ref[:, pl.ds(pl.multiple_of(block * 128, 128), 128)], prow[...], 0, 0)
            if k:
                lsrc[block] = part
                xcopy(1, k, lsrc.at[block], lxrecv.at[x]).start()
            else:
                lxrecv[x] = part
        group("lx", xcopy, 1, lxrecv.at[pl.ds(0, 3)])

    def share_panel():
        recv("pone")
        pall[cix] = pone[...]
        zloop(lambda k: zcopy(7, k, pall.at[cix], pall.at[cix]).start())
        group("pall", zcopy, 7, pall.at[pl.ds(0, 15)])
        recv("tblock")

        @pl.when(y == 0)
        def _():
            for k in range(1, NY):
                ycopy(0, k, rows(tblock, k, 16), tchunk).start()
            tchunk[...] = tblock[0:16, :]
        begin("tchunk", only(y != 0, landed(ycopy, 0, tchunk)), only(y == 0, left(ycopy, 0, tblock.at[pl.ds(0, 112)])))

    def share_x():
        recv("aleft")
        recv("x")
        xall[cix, :, :n] = jnp.sum(xrecv[...], axis=0)
        xall[cix, :, n:] = aleft[...]
        zloop(lambda k: zcopy(5, k, xall.at[cix], xall.at[cix]).start())
        group("xall", zcopy, 5, xall.at[pl.ds(0, 15)])

    def at(name):
        for b, f in ((PLACE['pass'], pass_panel), (PLACE['l'], send_l), (PLACE['sx'], share_x), (PLACE['sp'], share_panel)):
            if b == name:
                f()

    at(-2)
    recv("gall")
    at(-1)
    work[:, :n] = gall[...].reshape(n, n)
    work[:, n:] = identity(n)
    factor(work, {b: functools.partial(at, b) for b in range(16)})
    at(16)

    recv("lx")
    lysrc[...] = jnp.sum(lxrecv[...], axis=0)
    for k in range(1, NY):
        ycopy(1, k, rows(lysrc, lax.rem(y + k, NY), 16), lyrecv.at[y]).start()
    lyrecv[y] = lysrc[pl.ds(pl.multiple_of(y * 16, 16), 16), :]
    group("ly", ycopy, 1, lyrecv.at[pl.ds(0, 7)])

    eye = identity(n)
    first = (cix == 0).astype(F)
    top = (rix == 0).astype(F)
    t = work[:, n:]
    yrow = dot(prow[...], t, 1, 1)
    yrow = jnp.concatenate([yrow[:n] + top * eye, yrow[n:]], 0)
    recv("pall")
    s = inverse(dot(pall[...].reshape(n, n), t, 1, 1), PLACE['nd'])
    ycol = dot(p_ref[...], t, 1, 1)
    ycol = jnp.concatenate([ycol[:n] + first * eye, ycol[n:]], 0)
    vt = dot(ycol, s, 1, 1)
    vts[...] = vt.reshape(4, n, n)
    ys = dot(yrow, s, 1, 1)
    recv("xall")
    xa = xall[...].reshape(256, 2 * n)
    nrow = dot(xa[:, :n], t, 1, 1) + xa[:, n:]
    zown[...] = dot(yrow, nrow, 0, 0)
    zy[y] = zown[pl.ds(pl.multiple_of(cix * 8, 8), 8), :]
    for k in range(1, NY):
        ycopy(2, k, zy.at[y], zy.at[y]).start()
    group("zy", ycopy, 2, zy.at[pl.ds(0, 7)])
    upper = lax.broadcasted_iota(jnp.int32, (n, n), 0) <= lax.broadcasted_iota(jnp.int32, (n, n), 1)
    band_ref[...] = jnp.where(upper, -work[:, :n], 0.0)

    def gather_y():
        recv("tchunk")
        recv("ly")
        part = mall.at[x, pl.ds(pl.multiple_of(y * 16, 16), 16)]
        part[...] = dot(jnp.sum(lyrecv[...], axis=0), work[:, n:], 1, 1) + tchunk[...]
        for k in range(1, NY):
            mcopy(k, part, part).start()
        for k in range(1, NX):
            fcopy(0, k, part, part).start()
        for k in range(1, NY):
            begin(f"m{k}", mcopy(k, tchunk, tchunk).wait_recv, lambda: None)
        waits["m1"][1] = left(ycopy, 3, tblock.at[pl.ds(0, 112)])

    def z_x():
        recv("zy")
        zx[x] = jnp.sum(zy[...], axis=0)
        for k in range(1, NX):
            xcopy(2, k, zx.at[x], zx.at[x]).start()
        group("zx", xcopy, 2, zx.at[pl.ds(0, 3)])

    def z_col():
        recv("zx")
        zall[cix] = jnp.sum(zx[...], axis=0)
        zloop(lambda k: zcopy(6, k, zall.at[cix], zall.at[cix]).start())
        group("zall", zcopy, 6, zall.at[pl.ds(0, 15)])

    def gather_x(j):
        def go():
            part = mall.at[x, pl.ds(pl.multiple_of(lax.rem(y + NY - j, NY) * 16, 16), 16)]
            recv(f"m{j}")
            for k in range(1, NX):
                fcopy(j, k, part, part).start()
        return go

    gather_y()
    for j in PLACE['g1']:
        gather_x(j)()
    z_x()
    out_ref[...] = a_ref[...] - dot(nrow, vt, 1, 1)
    for j in PLACE['g2']:
        gather_x(j)()
    z_col()
    for j in PLACE['g3']:
        gather_x(j)()
    recv("zall")
    zfull = zall[...].reshape(n, n)
    for k in (0, 1, 3, 2):
        block = lax.rem(x + NX - k, NX)
        if k:
            fcopy(0, k, mall.at[0], mall.at[0]).wait_recv()
        rest = mall[block] - dot(vts[block], zfull, 1, 1)
        at_block = pl.ds(pl.multiple_of(block * 128, 128), 128)
        out_ref[:, at_block] = out_ref[:, at_block] - dot(ys, rest, 1, 1)

    drain()
    for k in range(1, NX):
        fcopy(0, k, mall.at[0], mall.at[0]).wait_send()


def per_device(matrix, panel):
    keep = lambda v: pltpu.with_memory_space_constraint(v, pltpu.MemorySpace.HBM)
    vm = lambda *shape: pltpu.VMEM(shape, F)
    dma = lambda *shape: pltpu.SemaphoreType.DMA(shape)
    return pl.pallas_call(
        kernel,
        out_shape=(jax.ShapeDtypeStruct((256, 512), F), jax.ShapeDtypeStruct((128, 128), F)),
        in_specs=[pl.BlockSpec(memory_space=pltpu.MemorySpace.HBM)] * 2,
        out_specs=(pl.BlockSpec(memory_space=pltpu.VMEM),) * 2,
        scratch_shapes=[
            vm(256, 512), vm(512, 128),
            vm(256, 128), vm(128, 128), vm(16, 8, 128), vm(8, 128), vm(16, 8, 128), vm(16, 8, 128),
            vm(256, 128), vm(16, 16, 128), vm(16, 128), vm(16, 16, 256),
            vm(4, 128, 128), vm(4, 128, 128), vm(128, 128), vm(8, 16, 128), vm(512, 128), vm(128, 128), vm(16, 128),
            vm(4, 128, 128), vm(128, 128), vm(8, 8, 128), vm(4, 8, 128), vm(16, 8, 128), vm(128, 256), vm(4, 128, 128),
            dma(8), dma(8), dma(3), dma(3), dma(4), dma(4), dma(3), dma(2), dma(4), dma(4), dma(8),
            dma(4), dma(4),
        ],
        compiler_params=pltpu.CompilerParams(collective_id=0, has_side_effects=True, vmem_limit_bytes=16 << 20),
        name="panel_transform",
    )(keep(matrix), keep(panel))


def solution(mesh):
    placed = (P("row", "col"), P("col", None))
    return jax.shard_map(
        per_device, mesh=mesh, in_specs=placed, out_specs=(P("row", "col"), P()), check_vma=False
    )
```

```python
import functools

PLACE = {'p': 0, 'x': 1, 'pass': 1, 'l': 3, 'sx': 7, 'sp': 0, 'nd': 14, 'g1': (), 'g2': (1, 7), 'g3': (2, 6, 3, 5, 4)}
import jax
import jax.numpy as jnp
from jax import lax
from jax.experimental import pallas as pl
from jax.experimental.pallas import tpu as pltpu
from jax.sharding import PartitionSpec as P

F = jnp.float32
MESH = pl.DeviceIdType.MESH
NX, NY, NC = 4, 8, 16


def split(v):
    high = v.astype(jnp.bfloat16).astype(F)
    rest = v - high
    mid = rest.astype(jnp.bfloat16).astype(F)
    return high, mid, rest - mid


def dot(a, b, ca=1, cb=0):
    if ca == 0:
        return lax.dot_general(
            a, b, (((ca,), (cb,)), ((), ())), precision=lax.Precision.HIGHEST, preferred_element_type=F
        )
    ah, am, al = [v.astype(jnp.bfloat16) for v in split(a)]
    bh, bm, bl = [v.astype(jnp.bfloat16) for v in split(b)]
    left = jnp.concatenate([ah, ah, am, am, ah, al], ca)
    right = jnp.concatenate([bh, bm, bh, bm, bl, bh], cb)
    return lax.dot_general(left, right, (((ca,), (cb,)), ((), ())), preferred_element_type=F)


def dot_short(a, b):
    ah, am, al = split(a)
    bh, bm, bl = split(b)
    left = jnp.concatenate([ah, ah, am, am, ah, al], 0).astype(jnp.bfloat16)
    right = jnp.concatenate([bh, bm, bh, bm, bl, bh], 0).astype(jnp.bfloat16)
    return lax.dot_general(left, right, (((0,), (0,)), ((), ())), preferred_element_type=F)


def spread(v, i):
    return jnp.broadcast_to(v[i : i + 1, :], v.shape)


def identity(n):
    return (
        lax.broadcasted_iota(jnp.int32, (n, n), 0) == lax.broadcasted_iota(jnp.int32, (n, n), 1)
    ).astype(F)


def factor(m_ref, hooks):
    n = m_ref.shape[0]
    sub = lax.broadcasted_iota(jnp.int32, (8, n), 0)
    for b in range(n // 8):
        lo = 8 * b
        left = m_ref[lo : lo + 8, :n]
        right = m_ref[lo : lo + 8, n:]
        cols = [jnp.broadcast_to(left[:, lo + k : lo + k + 1], (8, n)) for k in range(8)]
        pivots = jnp.ones((8, n), F)
        for i in range(8):
            pivot = spread(cols[i], i)
            pivots = jnp.where(sub == i, pivot, pivots)
            if i < 7:
                mult = jnp.where(sub > i, cols[i] / pivot, 0.0)
                for k in range(i + 1, 8):
                    cols[k] = cols[k] - mult * spread(cols[k], i)
                left = left - mult * spread(left, i)
                right = right - mult * spread(right, i)
        scale = lax.rsqrt(pivots)
        left = left * scale
        both = jnp.concatenate([left, right * scale], 1)
        m_ref[lo : lo + 8, :] = both
        if lo + 8 < n:
            m_ref[lo + 8 :, :] = m_ref[lo + 8 :, :] - dot_short(left, both)[lo + 8 :]
        if b in hooks:
            hooks[b]()


def inverse(q, doublings):
    eye = identity(q.shape[0])
    power = 0.5 * (eye - q)
    total = 0.5 * (eye + power)
    for _ in range(doublings - 1):
        power = dot(power, power)
        total = total + dot(total, power)
    return total


def kernel(
    a_hbm, p_hbm, out_ref, band_ref,
    a_ref, p_ref, prow, gsrc, grecv, pone, pall, gall, xsrc, xrecv, aleft, xall,
    lsrc, lxrecv, lysrc, lyrecv, tsrc, tblock, tchunk, mall, zown, zy, zx, zall, work, vts,
    zsend, zrecv, xsend, xrecv_sem, ysend, yrecv_sem, psend, precv, fsend, frecv, msem, asem, psem,
):
    n = p_ref.shape[1]
    rix, cix = lax.axis_index("row"), lax.axis_index("col")
    x, y = lax.div(rix, NY), lax.rem(rix, NY)
    z, core = lax.div(cix, 2), lax.rem(cix, 2)

    def zpeer(k):
        return lax.rem(cix + k, NC)

    def xpeer(k):
        return lax.rem(x + k, NX) * NY + y

    def ypeer(k):
        return x * NY + lax.rem(y + k, NY)

    def zcopy(ph, k, src, dst):
        return pltpu.make_async_remote_copy(
            src_ref=src, dst_ref=dst, send_sem=zsend.at[ph], recv_sem=zrecv.at[ph],
            device_id={"col": zpeer(k)}, device_id_type=MESH)

    def xcopy(ph, k, src, dst):
        return pltpu.make_async_remote_copy(
            src_ref=src, dst_ref=dst, send_sem=xsend.at[ph], recv_sem=xrecv_sem.at[ph],
            device_id={"row": xpeer(k)}, device_id_type=MESH)

    def ycopy(ph, k, src, dst):
        return pltpu.make_async_remote_copy(
            src_ref=src, dst_ref=dst, send_sem=ysend.at[ph], recv_sem=yrecv_sem.at[ph],
            device_id={"row": ypeer(k)}, device_id_type=MESH)

    def mcopy(k, src, dst):
        return pltpu.make_async_remote_copy(
            src_ref=src, dst_ref=dst, send_sem=ysend.at[3], recv_sem=msem.at[k],
            device_id={"row": ypeer(k)}, device_id_type=MESH)

    def fcopy(j, k, src, dst):
        return pltpu.make_async_remote_copy(
            src_ref=src, dst_ref=dst, send_sem=fsend.at[k], recv_sem=frecv.at[k],
            device_id={"row": xpeer(k)}, device_id_type=MESH)

    def zloop(body):
        for k in (8, 9, 7, 10, 6, 11, 5, 12, 4, 13, 3, 14, 2, 15, 1):
            body(k)

    def rows(ref, index, count):
        return ref.at[pl.ds(pl.multiple_of(index * count, count), count)]

    waits = {}

    def begin(name, recv, send):
        waits[name] = [recv, send]

    def recv(name):
        waits[name][0]()
        waits[name][0] = None

    def drain():
        for first_wait, last_wait in waits.values():
            if first_wait is not None:
                first_wait()
            last_wait()

    def landed(copy, ph, ref):
        return lambda: copy(ph, 1, ref, ref).wait_recv()

    def left(copy, ph, ref):
        return lambda: copy(ph, 1, ref, ref).wait_send()

    def group(name, copy, ph, ref):
        begin(name, landed(copy, ph, ref), left(copy, ph, ref))

    def only(cond, f):
        return lambda: pl.when(cond)(f)

    pin = [pltpu.make_async_copy(p_hbm.at[pl.ds(128 * k, 128)], p_ref.at[pl.ds(128 * k, 128)], psem.at[k]) for k in range(4)]
    ain = [pltpu.make_async_copy(a_hbm.at[pl.ds(64 * k, 64)], a_ref.at[pl.ds(64 * k, 64)], asem.at[k]) for k in range(4)]
    for copy in pin + ain:
        copy.start()
    barrier = pltpu.get_barrier_semaphore()
    zloop(lambda k: pl.semaphore_signal(barrier, inc=1, device_id={"col": zpeer(k)}, device_id_type=MESH))
    for k in range(1, NX):
        pl.semaphore_signal(barrier, inc=1, device_id={"row": xpeer(k)}, device_id_type=MESH)
    for k in range(1, NY):
        pl.semaphore_signal(barrier, inc=1, device_id={"row": ypeer(k)}, device_id_type=MESH)
    for copy in pin:
        copy.wait()
    gsrc[...] = dot(p_ref[...], p_ref[...], 0, 0)
    grecv[cix] = gsrc[pl.ds(pl.multiple_of(cix * 8, 8), 8), :]
    for copy in ain:
        copy.wait()
    xsrc[...] = dot(a_ref[...], p_ref[...])
    xrecv[cix] = xsrc[pl.ds(pl.multiple_of(cix * 16, 16), 16), :]
    pl.semaphore_wait(barrier, NC - 1 + NX - 1 + NY - 1)

    zloop(lambda k: zcopy(2, k, rows(gsrc, zpeer(k), 8), grecv.at[cix]).start())
    group("gram", zcopy, 2, grecv.at[pl.ds(0, 15)])

    owner = lax.div(rix, 2)
    base = lax.rem(rix, 2) * 256
    oz = lax.div(owner, 2)

    def pcopy(slot, half_src, src, peer):
        return pltpu.make_async_remote_copy(
            src_ref=src, dst_ref=src if src is a_ref else rows(prow, half_src, 128), send_sem=psend.at[slot], recv_sem=precv.at[half_src],
            device_id={"col": peer}, device_id_type=MESH)

    def psource(half):
        return p_ref.at[pl.ds(pl.multiple_of(base + half * 128, 128), 128)]

    def send_panel():
        @pl.when(cix == owner)
        def _():
            for dz in (4, 5, 3, 6, 2, 7, 1):
                chip = lax.rem(z + dz, 8)
                for h in range(2):
                    pcopy(h, h, psource(h), chip * 2 + h).start()
            for h in range(2):
                pcopy(h, h, psource(h), z * 2 + 1 - core).start()
            prow[...] = p_ref[pl.ds(pl.multiple_of(base, 256), 256), :]

    def pass_panel():
        @pl.when(z != oz)
        def _():
            pcopy(0, core, rows(prow, core, 128), 0).wait_recv()
            pcopy(2, core, rows(prow, core, 128), z * 2 + 1 - core).start()

    def prow_recv():
        @pl.when(z != oz)
        def _():
            pcopy(0, 1 - core, rows(prow, 1 - core, 128), 0).wait_recv()

        @pl.when((z == oz) & (cix != owner))
        def _():
            for h in range(2):
                pcopy(0, h, rows(prow, h, 128), 0).wait_recv()

    def prow_send():
        @pl.when(cix == owner)
        def _():
            for h in range(2):
                pcopy(h, h, a_ref, 0).wait_send()

        @pl.when(z != oz)
        def _():
            pcopy(2, core, rows(prow, core, 128), 0).wait_send()

    begin("prow", prow_recv, prow_send)

    def send_leading():
        @pl.when(cix == 0)
        def _():
            zloop(lambda k: zcopy(0, k, rows(p_ref, zpeer(k), 8), pone).start())
            zloop(lambda k: zcopy(1, k, a_ref.at[pl.ds(pl.multiple_of(zpeer(k) * 16, 16), 16), pl.ds(0, 128)], aleft).start())
            pone[...] = p_ref[0:8, :]
            aleft[...] = a_ref[0:16, 0:128]

    begin("pone", only(cix != 0, landed(zcopy, 0, pone)), only(cix == 0, left(zcopy, 0, p_ref.at[pl.ds(0, 120)])))
    begin("aleft", only(cix != 0, landed(zcopy, 1, aleft)), only(cix == 0, left(zcopy, 1, xrecv.at[pl.ds(0, 15)])))

    def send_x():
        zloop(lambda k: zcopy(3, k, rows(xsrc, zpeer(k), 16), xrecv.at[cix]).start())
        group("x", zcopy, 3, xrecv.at[pl.ds(0, 15)])

    if PLACE['p'] == 0:
        send_panel()
    if PLACE['x'] == 0:
        send_leading()
        send_x()
    if PLACE['p'] == 2:
        send_panel()

    recv("gram")
    gall[cix] = jnp.sum(grecv[...], axis=0)
    zloop(lambda k: zcopy(4, k, gall.at[cix], gall.at[cix]).start())
    group("gall", zcopy, 4, gall.at[pl.ds(0, 15)])
    if PLACE['p'] == 1:
        send_panel()
    if PLACE['x'] == 1:
        send_leading()
        send_x()

    @pl.when(rix == 0)
    def _():
        tsrc[...] = a_ref[0:128, :].T
        for k in range(1, NX):
            xcopy(0, k, rows(tsrc, k, 128), tblock).start()
        tblock[...] = tsrc[0:128, :]
    begin("tblock", only((y == 0) & (x != 0), landed(xcopy, 0, tblock)), only(rix == 0, left(xcopy, 0, lxrecv.at[pl.ds(0, 3)])))

    def send_l():
        recv("prow")
        for k in (2, 1, 3, 0):
            block = lax.rem(x + k, NX)
            part = dot(a_ref[:, pl.ds(pl.multiple_of(block * 128, 128), 128)], prow[...], 0, 0)
            if k:
                lsrc[block] = part
                xcopy(1, k, lsrc.at[block], lxrecv.at[x]).start()
            else:
                lxrecv[x] = part
        group("lx", xcopy, 1, lxrecv.at[pl.ds(0, 3)])

    def share_panel():
        recv("pone")
        pall[cix] = pone[...]
        zloop(lambda k: zcopy(7, k, pall.at[cix], pall.at[cix]).start())
        group("pall", zcopy, 7, pall.at[pl.ds(0, 15)])
        recv("tblock")

        @pl.when(y == 0)
        def _():
            for k in range(1, NY):
                ycopy(0, k, rows(tblock, k, 16), tchunk).start()
            tchunk[...] = tblock[0:16, :]
        begin("tchunk", only(y != 0, landed(ycopy, 0, tchunk)), only(y == 0, left(ycopy, 0, tblock.at[pl.ds(0, 112)])))

    def share_x():
        recv("aleft")
        recv("x")
        xall[cix, :, :n] = jnp.sum(xrecv[...], axis=0)
        xall[cix, :, n:] = aleft[...]
        zloop(lambda k: zcopy(5, k, xall.at[cix], xall.at[cix]).start())
        group("xall", zcopy, 5, xall.at[pl.ds(0, 15)])

    def at(name):
        for b, f in ((PLACE['pass'], pass_panel), (PLACE['l'], send_l), (PLACE['sx'], share_x), (PLACE['sp'], share_panel)):
            if b == name:
                f()

    at(-2)
    recv("gall")
    at(-1)
    work[:, :n] = gall[...].reshape(n, n)
    work[:, n:] = identity(n)
    factor(work, {b: functools.partial(at, b) for b in range(16)})
    at(16)

    recv("lx")
    lysrc[...] = jnp.sum(lxrecv[...], axis=0)
    for k in range(1, NY):
        ycopy(1, k, rows(lysrc, lax.rem(y + k, NY), 16), lyrecv.at[y]).start()
    lyrecv[y] = lysrc[pl.ds(pl.multiple_of(y * 16, 16), 16), :]
    group("ly", ycopy, 1, lyrecv.at[pl.ds(0, 7)])

    eye = identity(n)
    first = (cix == 0).astype(F)
    top = (rix == 0).astype(F)
    t = work[:, n:]
    yrow = dot(prow[...], t, 1, 1)
    yrow = jnp.concatenate([yrow[:n] + top * eye, yrow[n:]], 0)
    recv("pall")
    s = inverse(dot(pall[...].reshape(n, n), t, 1, 1), PLACE['nd'])
    ycol = dot(p_ref[...], t, 1, 1)
    ycol = jnp.concatenate([ycol[:n] + first * eye, ycol[n:]], 0)
    vt = dot(ycol, s, 1, 1)
    vts[...] = vt.reshape(4, n, n)
    ys = dot(yrow, s, 1, 1)
    recv("xall")
    xa = xall[...].reshape(256, 2 * n)
    nrow = dot(xa[:, :n], t, 1, 1) + xa[:, n:]
    zown[...] = dot(yrow, nrow, 0, 0)
    zy[y] = zown[pl.ds(pl.multiple_of(cix * 8, 8), 8), :]
    for k in range(1, NY):
        ycopy(2, k, zy.at[y], zy.at[y]).start()
    group("zy", ycopy, 2, zy.at[pl.ds(0, 7)])
    upper = lax.broadcasted_iota(jnp.int32, (n, n), 0) <= lax.broadcasted_iota(jnp.int32, (n, n), 1)
    band_ref[...] = jnp.where(upper, -work[:, :n], 0.0)

    def gather_y():
        recv("tchunk")
        recv("ly")
        part = mall.at[x, pl.ds(pl.multiple_of(y * 16, 16), 16)]
        part[...] = dot(jnp.sum(lyrecv[...], axis=0), work[:, n:], 1, 1) + tchunk[...]
        for k in range(1, NY):
            mcopy(k, part, part).start()
        for k in range(1, NX):
            fcopy(0, k, part, part).start()
        for k in range(1, NY):
            begin(f"m{k}", mcopy(k, tchunk, tchunk).wait_recv, lambda: None)
        waits["m1"][1] = left(ycopy, 3, tblock.at[pl.ds(0, 112)])

    def z_x():
        recv("zy")
        zx[x] = jnp.sum(zy[...], axis=0)
        for k in range(1, NX):
            xcopy(2, k, zx.at[x], zx.at[x]).start()
        group("zx", xcopy, 2, zx.at[pl.ds(0, 3)])

    def z_col():
        recv("zx")
        zall[cix] = jnp.sum(zx[...], axis=0)
        zloop(lambda k: zcopy(6, k, zall.at[cix], zall.at[cix]).start())
        group("zall", zcopy, 6, zall.at[pl.ds(0, 15)])

    def gather_x(j):
        def go():
            part = mall.at[x, pl.ds(pl.multiple_of(lax.rem(y + NY - j, NY) * 16, 16), 16)]
            recv(f"m{j}")
            for k in range(1, NX):
                fcopy(j, k, part, part).start()
        return go

    z_x()
    gather_y()
    out_ref[...] = a_ref[...] - dot(nrow, vt, 1, 1)
    for j in PLACE['g2']:
        gather_x(j)()
    z_col()
    for j in PLACE['g3']:
        gather_x(j)()
    recv("zall")
    zfull = zall[...].reshape(n, n)
    for k in (0, 1, 3, 2):
        block = lax.rem(x + NX - k, NX)
        if k:
            fcopy(0, k, mall.at[0], mall.at[0]).wait_recv()
        rest = mall[block] - dot(vts[block], zfull, 1, 1)
        at_block = pl.ds(pl.multiple_of(block * 128, 128), 128)
        out_ref[:, at_block] = out_ref[:, at_block] - dot(ys, rest, 1, 1)

    drain()
    for k in range(1, NX):
        fcopy(0, k, mall.at[0], mall.at[0]).wait_send()


def per_device(matrix, panel):
    keep = lambda v: pltpu.with_memory_space_constraint(v, pltpu.MemorySpace.HBM)
    vm = lambda *shape: pltpu.VMEM(shape, F)
    dma = lambda *shape: pltpu.SemaphoreType.DMA(shape)
    return pl.pallas_call(
        kernel,
        out_shape=(jax.ShapeDtypeStruct((256, 512), F), jax.ShapeDtypeStruct((128, 128), F)),
        in_specs=[pl.BlockSpec(memory_space=pltpu.MemorySpace.HBM)] * 2,
        out_specs=(pl.BlockSpec(memory_space=pltpu.VMEM),) * 2,
        scratch_shapes=[
            vm(256, 512), vm(512, 128),
            vm(256, 128), vm(128, 128), vm(16, 8, 128), vm(8, 128), vm(16, 8, 128), vm(16, 8, 128),
            vm(256, 128), vm(16, 16, 128), vm(16, 128), vm(16, 16, 256),
            vm(4, 128, 128), vm(4, 128, 128), vm(128, 128), vm(8, 16, 128), vm(512, 128), vm(128, 128), vm(16, 128),
            vm(4, 128, 128), vm(128, 128), vm(8, 8, 128), vm(4, 8, 128), vm(16, 8, 128), vm(128, 256), vm(4, 128, 128),
            dma(8), dma(8), dma(3), dma(3), dma(4), dma(4), dma(3), dma(2), dma(4), dma(4), dma(8),
            dma(4), dma(4),
        ],
        compiler_params=pltpu.CompilerParams(collective_id=0, has_side_effects=True, vmem_limit_bytes=16 << 20),
        name="panel_transform",
    )(keep(matrix), keep(panel))


def solution(mesh):
    placed = (P("row", "col"), P("col", None))
    return jax.shard_map(
        per_device, mesh=mesh, in_specs=placed, out_specs=(P("row", "col"), P()), check_vma=False
    )
```

```python
import functools

PLACE = {'p': 0, 'x': 1, 'pass': 1, 'l': 3, 'sx': 7, 'sp': 0, 'nd': 14, 'g1': (), 'g2': (1, 7), 'g3': (2, 6, 3, 5, 4)}
import jax
import jax.numpy as jnp
from jax import lax
from jax.experimental import pallas as pl
from jax.experimental.pallas import tpu as pltpu
from jax.sharding import PartitionSpec as P

F = jnp.float32
MESH = pl.DeviceIdType.MESH
NX, NY, NC = 4, 8, 16


def split(v):
    high = v.astype(jnp.bfloat16).astype(F)
    rest = v - high
    mid = rest.astype(jnp.bfloat16).astype(F)
    return high, mid, rest - mid


def dot(a, b, ca=1, cb=0):
    if ca == 0:
        return lax.dot_general(
            a, b, (((ca,), (cb,)), ((), ())), precision=lax.Precision.HIGHEST, preferred_element_type=F
        )
    ah, am, al = [v.astype(jnp.bfloat16) for v in split(a)]
    bh, bm, bl = [v.astype(jnp.bfloat16) for v in split(b)]
    left = jnp.concatenate([ah, ah, am, am, ah, al], ca)
    right = jnp.concatenate([bh, bm, bh, bm, bl, bh], cb)
    return lax.dot_general(left, right, (((ca,), (cb,)), ((), ())), preferred_element_type=F)


def dot_short(a, b):
    ah, am, al = split(a)
    bh, bm, bl = split(b)
    left = jnp.concatenate([ah, ah, am, am, ah, al], 0).astype(jnp.bfloat16)
    right = jnp.concatenate([bh, bm, bh, bm, bl, bh], 0).astype(jnp.bfloat16)
    return lax.dot_general(left, right, (((0,), (0,)), ((), ())), preferred_element_type=F)


def spread(v, i):
    return jnp.broadcast_to(v[i : i + 1, :], v.shape)


def identity(n):
    return (
        lax.broadcasted_iota(jnp.int32, (n, n), 0) == lax.broadcasted_iota(jnp.int32, (n, n), 1)
    ).astype(F)


def factor(m_ref, hooks):
    n = m_ref.shape[0]
    sub = lax.broadcasted_iota(jnp.int32, (8, n), 0)
    for b in range(n // 8):
        lo = 8 * b
        left = m_ref[lo : lo + 8, :n]
        right = m_ref[lo : lo + 8, n:]
        cols = [jnp.broadcast_to(left[:, lo + k : lo + k + 1], (8, n)) for k in range(8)]
        pivots = jnp.ones((8, n), F)
        for i in range(8):
            pivot = spread(cols[i], i)
            pivots = jnp.where(sub == i, pivot, pivots)
            if i < 7:
                mult = jnp.where(sub > i, cols[i] / pivot, 0.0)
                for k in range(i + 1, 8):
                    cols[k] = cols[k] - mult * spread(cols[k], i)
                left = left - mult * spread(left, i)
                right = right - mult * spread(right, i)
        scale = lax.rsqrt(pivots)
        left = left * scale
        both = jnp.concatenate([left, right * scale], 1)
        m_ref[lo : lo + 8, :] = both
        if lo + 8 < n:
            m_ref[lo + 8 :, :] = m_ref[lo + 8 :, :] - dot_short(left, both)[lo + 8 :]
        if b in hooks:
            hooks[b]()


def inverse(q, doublings):
    eye = identity(q.shape[0])
    power = 0.5 * (eye - q)
    total = 0.5 * (eye + power)
    for _ in range(doublings - 1):
        power = dot(power, power)
        total = total + dot(total, power)
    return total


def kernel(
    a_hbm, p_hbm, out_ref, band_ref,
    a_ref, p_ref, prow, gsrc, grecv, pone, pall, gall, xsrc, xrecv, aleft, xall,
    lsrc, lxrecv, lysrc, lyrecv, tsrc, tblock, tchunk, mall, zown, zy, zx, zall, work, vts,
    zsend, zrecv, xsend, xrecv_sem, ysend, yrecv_sem, psend, precv, fsend, frecv, msem, asem, psem,
):
    n = p_ref.shape[1]
    rix, cix = lax.axis_index("row"), lax.axis_index("col")
    x, y = lax.div(rix, NY), lax.rem(rix, NY)
    z, core = lax.div(cix, 2), lax.rem(cix, 2)

    def zpeer(k):
        return lax.rem(cix + k, NC)

    def xpeer(k):
        return lax.rem(x + k, NX) * NY + y

    def ypeer(k):
        return x * NY + lax.rem(y + k, NY)

    def zcopy(ph, k, src, dst):
        return pltpu.make_async_remote_copy(
            src_ref=src, dst_ref=dst, send_sem=zsend.at[ph], recv_sem=zrecv.at[ph],
            device_id={"col": zpeer(k)}, device_id_type=MESH)

    def xcopy(ph, k, src, dst):
        return pltpu.make_async_remote_copy(
            src_ref=src, dst_ref=dst, send_sem=xsend.at[ph], recv_sem=xrecv_sem.at[ph],
            device_id={"row": xpeer(k)}, device_id_type=MESH)

    def ycopy(ph, k, src, dst):
        return pltpu.make_async_remote_copy(
            src_ref=src, dst_ref=dst, send_sem=ysend.at[ph], recv_sem=yrecv_sem.at[ph],
            device_id={"row": ypeer(k)}, device_id_type=MESH)

    def mcopy(k, src, dst):
        return pltpu.make_async_remote_copy(
            src_ref=src, dst_ref=dst, send_sem=ysend.at[3], recv_sem=msem.at[k],
            device_id={"row": ypeer(k)}, device_id_type=MESH)

    def fcopy(j, k, src, dst):
        return pltpu.make_async_remote_copy(
            src_ref=src, dst_ref=dst, send_sem=fsend.at[k], recv_sem=frecv.at[k],
            device_id={"row": xpeer(k)}, device_id_type=MESH)

    def zloop(body):
        for k in (8, 9, 7, 10, 6, 11, 5, 12, 4, 13, 3, 14, 2, 15, 1):
            body(k)

    def rows(ref, index, count):
        return ref.at[pl.ds(pl.multiple_of(index * count, count), count)]

    waits = {}

    def begin(name, recv, send):
        waits[name] = [recv, send]

    def recv(name):
        waits[name][0]()
        waits[name][0] = None

    def drain():
        for first_wait, last_wait in waits.values():
            if first_wait is not None:
                first_wait()
            last_wait()

    def landed(copy, ph, ref):
        return lambda: copy(ph, 1, ref, ref).wait_recv()

    def left(copy, ph, ref):
        return lambda: copy(ph, 1, ref, ref).wait_send()

    def group(name, copy, ph, ref):
        begin(name, landed(copy, ph, ref), left(copy, ph, ref))

    def only(cond, f):
        return lambda: pl.when(cond)(f)

    pin = [pltpu.make_async_copy(p_hbm.at[pl.ds(128 * k, 128)], p_ref.at[pl.ds(128 * k, 128)], psem.at[k]) for k in range(4)]
    ain = [pltpu.make_async_copy(a_hbm.at[pl.ds(64 * k, 64)], a_ref.at[pl.ds(64 * k, 64)], asem.at[k]) for k in range(4)]
    for copy in pin + ain:
        copy.start()
    barrier = pltpu.get_barrier_semaphore()
    zloop(lambda k: pl.semaphore_signal(barrier, inc=1, device_id={"col": zpeer(k)}, device_id_type=MESH))
    for k in range(1, NX):
        pl.semaphore_signal(barrier, inc=1, device_id={"row": xpeer(k)}, device_id_type=MESH)
    for k in range(1, NY):
        pl.semaphore_signal(barrier, inc=1, device_id={"row": ypeer(k)}, device_id_type=MESH)
    for copy in pin:
        copy.wait()
    gsrc[...] = dot(p_ref[...], p_ref[...], 0, 0)
    grecv[cix] = gsrc[pl.ds(pl.multiple_of(cix * 8, 8), 8), :]
    for copy in ain:
        copy.wait()
    xsrc[...] = dot(a_ref[...], p_ref[...])
    xrecv[cix] = xsrc[pl.ds(pl.multiple_of(cix * 16, 16), 16), :]
    pl.semaphore_wait(barrier, NC - 1 + NX - 1 + NY - 1)

    zloop(lambda k: zcopy(2, k, rows(gsrc, zpeer(k), 8), grecv.at[cix]).start())
    group("gram", zcopy, 2, grecv.at[pl.ds(0, 15)])

    owner = lax.div(rix, 2)
    base = lax.rem(rix, 2) * 256
    oz = lax.div(owner, 2)

    def pcopy(slot, half_src, src, peer):
        return pltpu.make_async_remote_copy(
            src_ref=src, dst_ref=src if src is a_ref else rows(prow, half_src, 128), send_sem=psend.at[slot], recv_sem=precv.at[half_src],
            device_id={"col": peer}, device_id_type=MESH)

    def psource(half):
        return p_ref.at[pl.ds(pl.multiple_of(base + half * 128, 128), 128)]

    def send_panel():
        @pl.when(cix == owner)
        def _():
            for dz in (4, 5, 3, 6, 2, 7, 1):
                chip = lax.rem(z + dz, 8)
                for h in range(2):
                    pcopy(h, h, psource(h), chip * 2 + h).start()
            for h in range(2):
                pcopy(h, h, psource(h), z * 2 + 1 - core).start()
            prow[...] = p_ref[pl.ds(pl.multiple_of(base, 256), 256), :]

    def pass_panel():
        @pl.when(z != oz)
        def _():
            pcopy(0, core, rows(prow, core, 128), 0).wait_recv()
            pcopy(2, core, rows(prow, core, 128), z * 2 + 1 - core).start()

    def prow_recv():
        @pl.when(z != oz)
        def _():
            pcopy(0, 1 - core, rows(prow, 1 - core, 128), 0).wait_recv()

        @pl.when((z == oz) & (cix != owner))
        def _():
            for h in range(2):
                pcopy(0, h, rows(prow, h, 128), 0).wait_recv()

    def prow_send():
        @pl.when(cix == owner)
        def _():
            for h in range(2):
                pcopy(h, h, a_ref, 0).wait_send()

        @pl.when(z != oz)
        def _():
            pcopy(2, core, rows(prow, core, 128), 0).wait_send()

    begin("prow", prow_recv, prow_send)

    def send_leading():
        @pl.when(cix == 0)
        def _():
            zloop(lambda k: zcopy(0, k, rows(p_ref, zpeer(k), 8), pone).start())
            zloop(lambda k: zcopy(1, k, a_ref.at[pl.ds(pl.multiple_of(zpeer(k) * 16, 16), 16), pl.ds(0, 128)], aleft).start())
            pone[...] = p_ref[0:8, :]
            aleft[...] = a_ref[0:16, 0:128]

    begin("pone", only(cix != 0, landed(zcopy, 0, pone)), only(cix == 0, left(zcopy, 0, p_ref.at[pl.ds(0, 120)])))
    begin("aleft", only(cix != 0, landed(zcopy, 1, aleft)), only(cix == 0, left(zcopy, 1, xrecv.at[pl.ds(0, 15)])))

    def send_x():
        zloop(lambda k: zcopy(3, k, rows(xsrc, zpeer(k), 16), xrecv.at[cix]).start())
        group("x", zcopy, 3, xrecv.at[pl.ds(0, 15)])

    if PLACE['p'] == 0:
        send_panel()
    if PLACE['x'] == 0:
        send_leading()
        send_x()
    if PLACE['p'] == 2:
        send_panel()

    recv("gram")
    gall[cix] = jnp.sum(grecv[...], axis=0)
    zloop(lambda k: zcopy(4, k, gall.at[cix], gall.at[cix]).start())
    group("gall", zcopy, 4, gall.at[pl.ds(0, 15)])
    if PLACE['p'] == 1:
        send_panel()
    if PLACE['x'] == 1:
        send_leading()
        send_x()

    @pl.when(rix == 0)
    def _():
        tsrc[...] = a_ref[0:128, :].T
        for k in range(1, NX):
            xcopy(0, k, rows(tsrc, k, 128), tblock).start()
        tblock[...] = tsrc[0:128, :]
    begin("tblock", only((y == 0) & (x != 0), landed(xcopy, 0, tblock)), only(rix == 0, left(xcopy, 0, lxrecv.at[pl.ds(0, 3)])))

    def send_l():
        recv("prow")
        for k in (2, 1, 3, 0):
            block = lax.rem(x + k, NX)
            part = dot(a_ref[:, pl.ds(pl.multiple_of(block * 128, 128), 128)], prow[...], 0, 0)
            if k:
                lsrc[block] = part
                xcopy(1, k, lsrc.at[block], lxrecv.at[x]).start()
            else:
                lxrecv[x] = part
        group("lx", xcopy, 1, lxrecv.at[pl.ds(0, 3)])

    def share_panel():
        recv("pone")
        pall[cix] = pone[...]
        zloop(lambda k: zcopy(7, k, pall.at[cix], pall.at[cix]).start())
        group("pall", zcopy, 7, pall.at[pl.ds(0, 15)])
        recv("tblock")

        @pl.when(y == 0)
        def _():
            for k in range(1, NY):
                ycopy(0, k, rows(tblock, k, 16), tchunk).start()
            tchunk[...] = tblock[0:16, :]
        begin("tchunk", only(y != 0, landed(ycopy, 0, tchunk)), only(y == 0, left(ycopy, 0, tblock.at[pl.ds(0, 112)])))

    def share_x():
        recv("aleft")
        recv("x")
        xall[cix, :, :n] = jnp.sum(xrecv[...], axis=0)
        xall[cix, :, n:] = aleft[...]
        zloop(lambda k: zcopy(5, k, xall.at[cix], xall.at[cix]).start())
        group("xall", zcopy, 5, xall.at[pl.ds(0, 15)])

    def at(name):
        for b, f in ((PLACE['pass'], pass_panel), (PLACE['l'], send_l), (PLACE['sx'], share_x), (PLACE['sp'], share_panel)):
            if b == name:
                f()

    at(-2)
    recv("gall")
    at(-1)
    work[:, :n] = gall[...].reshape(n, n)
    work[:, n:] = identity(n)
    factor(work, {b: functools.partial(at, b) for b in range(16)})
    at(16)

    recv("lx")
    lysrc[...] = jnp.sum(lxrecv[...], axis=0)
    for k in range(1, NY):
        ycopy(1, k, rows(lysrc, lax.rem(y + k, NY), 16), lyrecv.at[y]).start()
    lyrecv[y] = lysrc[pl.ds(pl.multiple_of(y * 16, 16), 16), :]
    group("ly", ycopy, 1, lyrecv.at[pl.ds(0, 7)])

    eye = identity(n)
    first = (cix == 0).astype(F)
    top = (rix == 0).astype(F)
    t = work[:, n:]
    yrow = dot(prow[...], t, 1, 1)
    yrow = jnp.concatenate([yrow[:n] + top * eye, yrow[n:]], 0)
    recv("pall")
    s = inverse(dot(pall[...].reshape(n, n), t, 1, 1), PLACE['nd'])
    ycol = dot(p_ref[...], t, 1, 1)
    ycol = jnp.concatenate([ycol[:n] + first * eye, ycol[n:]], 0)
    recv("xall")
    xa = xall[...].reshape(256, 2 * n)
    nrow = dot(xa[:, :n], t, 1, 1) + xa[:, n:]
    zown[...] = dot(yrow, nrow, 0, 0)
    zy[y] = zown[pl.ds(pl.multiple_of(cix * 8, 8), 8), :]
    for k in range(1, NY):
        ycopy(2, k, zy.at[y], zy.at[y]).start()
    group("zy", ycopy, 2, zy.at[pl.ds(0, 7)])
    vt = dot(ycol, s, 1, 1)
    vts[...] = vt.reshape(4, n, n)
    ys = dot(yrow, s, 1, 1)
    upper = lax.broadcasted_iota(jnp.int32, (n, n), 0) <= lax.broadcasted_iota(jnp.int32, (n, n), 1)
    band_ref[...] = jnp.where(upper, -work[:, :n], 0.0)

    def gather_y():
        recv("tchunk")
        recv("ly")
        part = mall.at[x, pl.ds(pl.multiple_of(y * 16, 16), 16)]
        part[...] = dot(jnp.sum(lyrecv[...], axis=0), work[:, n:], 1, 1) + tchunk[...]
        for k in range(1, NY):
            mcopy(k, part, part).start()
        for k in range(1, NX):
            fcopy(0, k, part, part).start()
        for k in range(1, NY):
            begin(f"m{k}", mcopy(k, tchunk, tchunk).wait_recv, lambda: None)
        waits["m1"][1] = left(ycopy, 3, tblock.at[pl.ds(0, 112)])

    def z_x():
        recv("zy")
        zx[x] = jnp.sum(zy[...], axis=0)
        for k in range(1, NX):
            xcopy(2, k, zx.at[x], zx.at[x]).start()
        group("zx", xcopy, 2, zx.at[pl.ds(0, 3)])

    def z_col():
        recv("zx")
        zall[cix] = jnp.sum(zx[...], axis=0)
        zloop(lambda k: zcopy(6, k, zall.at[cix], zall.at[cix]).start())
        group("zall", zcopy, 6, zall.at[pl.ds(0, 15)])

    def gather_x(j):
        def go():
            part = mall.at[x, pl.ds(pl.multiple_of(lax.rem(y + NY - j, NY) * 16, 16), 16)]
            recv(f"m{j}")
            for k in range(1, NX):
                fcopy(j, k, part, part).start()
        return go

    z_x()
    gather_y()
    out_ref[...] = a_ref[...] - dot(nrow, vt, 1, 1)
    for j in PLACE['g2']:
        gather_x(j)()
    z_col()
    for j in PLACE['g3']:
        gather_x(j)()
    recv("zall")
    zfull = zall[...].reshape(n, n)
    for k in (0, 1, 3, 2):
        block = lax.rem(x + NX - k, NX)
        if k:
            fcopy(0, k, mall.at[0], mall.at[0]).wait_recv()
        rest = mall[block] - dot(vts[block], zfull, 1, 1)
        at_block = pl.ds(pl.multiple_of(block * 128, 128), 128)
        out_ref[:, at_block] = out_ref[:, at_block] - dot(ys, rest, 1, 1)

    drain()
    for k in range(1, NX):
        fcopy(0, k, mall.at[0], mall.at[0]).wait_send()


def per_device(matrix, panel):
    keep = lambda v: pltpu.with_memory_space_constraint(v, pltpu.MemorySpace.HBM)
    vm = lambda *shape: pltpu.VMEM(shape, F)
    dma = lambda *shape: pltpu.SemaphoreType.DMA(shape)
    return pl.pallas_call(
        kernel,
        out_shape=(jax.ShapeDtypeStruct((256, 512), F), jax.ShapeDtypeStruct((128, 128), F)),
        in_specs=[pl.BlockSpec(memory_space=pltpu.MemorySpace.HBM)] * 2,
        out_specs=(pl.BlockSpec(memory_space=pltpu.VMEM),) * 2,
        scratch_shapes=[
            vm(256, 512), vm(512, 128),
            vm(256, 128), vm(128, 128), vm(16, 8, 128), vm(8, 128), vm(16, 8, 128), vm(16, 8, 128),
            vm(256, 128), vm(16, 16, 128), vm(16, 128), vm(16, 16, 256),
            vm(4, 128, 128), vm(4, 128, 128), vm(128, 128), vm(8, 16, 128), vm(512, 128), vm(128, 128), vm(16, 128),
            vm(4, 128, 128), vm(128, 128), vm(8, 8, 128), vm(4, 8, 128), vm(16, 8, 128), vm(128, 256), vm(4, 128, 128),
            dma(8), dma(8), dma(3), dma(3), dma(4), dma(4), dma(3), dma(2), dma(4), dma(4), dma(8),
            dma(4), dma(4),
        ],
        compiler_params=pltpu.CompilerParams(collective_id=0, has_side_effects=True, vmem_limit_bytes=16 << 20),
        name="panel_transform",
    )(keep(matrix), keep(panel))


def solution(mesh):
    placed = (P("row", "col"), P("col", None))
    return jax.shard_map(
        per_device, mesh=mesh, in_specs=placed, out_specs=(P("row", "col"), P()), check_vma=False
    )
```
